256 devices in a mesh: row: 32 (over z, x_lo, core), col: 8 (over y, x_hi).
Axes of the slice: x: 4 (x_hi: 2, x_lo: 2; x = x_hi * 2 + x_lo), y: 4, z: 8, core: 2. Of those that a mesh axis runs over, the one named last changes fastest.
Arguments:
- samples: float32 [4194304], P(('row', 'col')), may hold values from -6 to 6
- stem_weight: float32 [32, 128], replicated, may hold values from -1 to 1
- in_weight: float32 [128, 384], replicated, may hold values from -0.5 to 0.5
- filter_param: float32 [262144, 128], P(('row', 'col')), may hold values from -6 to 6
- out_weight: float32 [128, 128], replicated, may hold values from -0.5 to 0.5
- cotangent: float32 [262144, 128], P(('row', 'col')), may hold values from -6 to 6
Outputs:
- layer_out: float32 [262144, 128], P(('row', 'col'))
- filter_grad: float32 [262144, 128], P(('row', 'col'))
- stem_grad: float32 [32, 128], replicated
- in_grad: float32 [128, 384], replicated
- out_grad: float32 [128, 128], replicated
The draws below stay inside these ranges and needn't reach their ends.
All inputs are finite; a program needn't handle non-finite values.
Results may differ from the reference program's by a relative error of at most 0.0008.
Values sent between devices are 32-bit elements; how exact they have to be, the bound alone decides.
A program may use at most 128 MiB of HBM per device.

```python
import math
import jax
import jax.numpy as jnp
from jax import lax

CHAN = 128
STRIDE = 16
FRAMES = 262144


def block_levels(own_key, shape, split, smallest, high):
    def one(dim, blocks):
        heights = jax.random.uniform(jax.random.fold_in(jax.random.fold_in(own_key, 6), dim), (blocks,), jnp.float32, smallest / len(split), high / len(split))
        return jnp.repeat(jnp.exp(heights), shape[dim] // blocks).reshape((-1,) + (1,) * (len(shape) - dim - 1))

    factor_of = one(*split[0])
    for cut in split[1:]:
        factor_of = factor_of * one(*cut)
    return factor_of


def gaussian(stream_key, shape, width, limit, split=(), held_as=jnp.bfloat16):
    result = width * jax.random.normal(stream_key, shape, jnp.float32)
    if split:
        result = result * block_levels(stream_key, shape, split, -0.22, 0.18)
    return jnp.clip(result, -limit, limit).astype(held_as)


def setup_inputs(seed: int = 0) -> dict:
    key_list = jax.random.split(jax.random.key(seed), 7)
    return {
        "samples": gaussian(key_list[0], (FRAMES * STRIDE,), 1.0, 6.0, ((0, 256),), jnp.float32),
        "stem_weight": gaussian(key_list[1], (2 * STRIDE, CHAN), (2 * STRIDE) ** -0.5, 1.0, (), jnp.float32),
        "in_weight": gaussian(key_list[2], (CHAN, 3 * CHAN), CHAN ** -0.5, 0.5, (), jnp.float32),
        "filter_param": gaussian(key_list[3], (FRAMES, CHAN), 1.0, 6.0, ((0, 256),), jnp.float32),
        "out_weight": gaussian(key_list[4], (CHAN, CHAN), CHAN ** -0.5, 0.5, (), jnp.float32),
        "cotangent": gaussian(key_list[5], (FRAMES, CHAN), 1.0, 6.0, ((0, 256),), jnp.float32),
    }


def reference(samples, stem_weight, in_weight, filter_param, out_weight, cotangent):
    scale = 1.0 / math.sqrt(FRAMES)
    padded = jnp.concatenate([samples, jnp.zeros((STRIDE,), samples.dtype)])
    windows = jnp.concatenate([samples.reshape(FRAMES, STRIDE), padded[STRIDE:].reshape(FRAMES, STRIDE)], axis=1)

    def forward(stem_w, in_w, filt, out_w):
        stem_out = jnp.dot(windows, stem_w, preferred_element_type=jnp.float32, precision=lax.Precision.HIGHEST)
        normed = stem_out * lax.rsqrt(lax.optimization_barrier(jnp.mean(stem_out * stem_out, axis=1, keepdims=True)) + 1e-05)
        projected = jnp.dot(normed, in_w, preferred_element_type=jnp.float32, precision=lax.Precision.HIGHEST)
        query_part = projected[:, :CHAN]
        key_part = projected[:, CHAN:2 * CHAN]
        value_part = projected[:, 2 * CHAN:]
        mixed_in = key_part * value_part
        filter_time = filt * scale
        spectrum = jnp.fft.rfft(mixed_in, axis=0) * jnp.fft.rfft(filter_time, axis=0)
        long_conv = jnp.fft.irfft(spectrum, n=FRAMES, axis=0)
        gated = query_part * long_conv
        return jnp.dot(gated, out_w, preferred_element_type=jnp.float32, precision=lax.Precision.HIGHEST) + stem_out
    layer_out, pullback = jax.vjp(forward, stem_weight, in_weight, filter_param, out_weight)
    stem_part, in_part, filter_grad, out_part = pullback(cotangent)
    return (layer_out, filter_grad, stem_part * scale, in_part * scale, out_part * scale)
```

```python
import math

import jax
import jax.numpy as jnp
from jax import lax
from jax.experimental import pallas as pl
from jax.experimental.pallas import tpu as pltpu
from jax.sharding import PartitionSpec as P

MESH = pl.DeviceIdType.MESH
F32 = jnp.float32
BF16 = jnp.bfloat16
EPSILON = 1e-05

CH = 128
LANE = 128
FR = 1024
HALF = 131072
ROWS = 528
CUT = 176
PIECE = 40
MEMBERS = 16

COS_TERMS = [(-1.0) ** i / math.factorial(2 * i) for i in range(9)]
SIN_TERMS = [(-1.0) ** i / math.factorial(2 * i + 1) for i in range(9)]


def split(x):
    high = x.astype(BF16)
    return high, (x - high.astype(F32)).astype(BF16)


def mm(a, b):
    return jnp.dot(a, b, preferred_element_type=F32)


def mm_nt(a, b):
    return lax.dot_general(a, b, (((1,), (1,)), ((), ())), preferred_element_type=F32)


def dot3(a, b, form=mm):
    (ah, al), (bh, bl) = a, b
    return form(ah, bh) + (form(al, bh) + form(ah, bl))


def sincos(index, period):
    half = period // 2
    x = (((index + half) & (period - 1)) - half).astype(F32) * (2.0 * math.pi / period)
    x2 = x * x
    c = jnp.full_like(x, COS_TERMS[-1])
    s = jnp.full_like(x, SIN_TERMS[-1])
    for term in COS_TERMS[-2::-1]:
        c = c * x2 + term
    for term in SIN_TERMS[-2::-1]:
        s = s * x2 + term
    return c, s * x


def iota(shape, dim):
    return lax.broadcasted_iota(jnp.int32, shape, dim)


def aligned(start, size, unit=8):
    return pl.ds(pl.multiple_of(start, unit), size)


def kernel(
    samples, stem_w, in_w, filt, out_w, cot,
    layer_out, filter_grad, stem_grad, in_grad, out_grad,
    s0, s1, s2, r0, r1, r2, x0, x1, x2, x3, x4, x5, c0, c1, c2, h0, h1, h2, o0, o1, o2,
    f1h, f1l, gh, gl, w2h, w2l, v2h, v2l, twc, tws,
    rhs2, yr, yi, spec,
    edge, win, stem, normed, qkv, gg,
    swh, swl, iwh, iwl, owh, owl,
    gsum, rs_in, red, ag_in, tot, fin,
    send_sem, recv_sem, xsend, xrecv, esend, erecv, rsend, rrecv,
):
    sbuf, rbuf, xbuf = (s0, s1, s2), (r0, r1, r2), (x0, x1, x2, x3, x4, x5)
    cbuf, hbuf, obuf = (c0, c1, c2), (h0, h1, h2), (o0, o1, o2)
    row, col = lax.axis_index("row"), lax.axis_index("col")
    core = row % 2
    half = row // 16
    chip = (row // 2) * 8 + col
    place = (row % 16) * 8 + col
    dev = row * 8 + col
    partner = (row + 1 - 2 * core, col)
    sign = (1 - 2 * core).astype(F32)
    own_half = half == core

    def tile(k):
        return aligned(k * 8, 8)

    def scatter(src, dst, unit, slot, own, target):
        def one(i, carry):
            k = (own + 1 + i) % CH
            pltpu.make_async_remote_copy(
                src.at[tile(k)], dst.at[tile(slot)], send_sem.at[unit], recv_sem.at[unit],
                device_id=target(k), device_id_type=MESH,
            ).start()
            return carry

        lax.fori_loop(0, CH - 1, one, 0)

        @pl.when(own_half)
        def _():
            pltpu.make_async_copy(src.at[tile(own)], dst.at[tile(slot)], recv_sem.at[unit]).start()

        @pl.when(jnp.logical_not(own_half))
        def _():
            pltpu.make_async_remote_copy(
                src.at[tile(own)], dst.at[tile(slot)], send_sem.at[unit], recv_sem.at[unit],
                device_id=target(own), device_id_type=MESH,
            ).start()

    def arrived(dst, unit):
        pltpu.make_async_copy(dst, dst, recv_sem.at[unit]).wait()

    def sent(src, unit):
        @pl.when(own_half)
        def _():
            part = src.at[pl.ds(0, FR - 8)]
            pltpu.make_async_copy(part, part, send_sem.at[unit]).wait()

        @pl.when(jnp.logical_not(own_half))
        def _():
            pltpu.make_async_copy(src, src, send_sem.at[unit]).wait()

    def to_chip(k):
        return ((k // 8) * 2 + half, k % 8)

    def to_frames(k):
        return (k // 8 + 16 * core, k % 8)

    def scatter_in(unit):
        scatter(sbuf[unit], rbuf[unit], unit, place, chip, to_chip)

    def scatter_out(unit):
        scatter(hbuf[unit], obuf[unit], 3 + unit, chip, place, to_frames)

    @pl.when(dev > 0)
    def _():
        pltpu.make_async_remote_copy(
            samples.at[pl.ds(0, 8)], edge, esend, erecv,
            device_id=((dev - 1) // 8, (dev + 7) % 8), device_id_type=MESH,
        ).start()

    def put_rows(unit, r, block):
        sbuf[unit][pl.ds(r, CH, stride=8), :] = block.T

    def filter_block(r, carry):
        put_rows(0, r, filt[aligned(r * LANE, LANE, LANE), :])
        return carry

    lax.fori_loop(0, 8, filter_block, 0)
    scatter_in(0)

    for src, high, low in ((stem_w, swh, swl), (in_w, iwh, iwl), (out_w, owh, owl)):
        h, l = split(src[...])
        high[...] = h
        low[...] = l

    @pl.when(dev == 255)
    def _():
        edge[...] = jnp.zeros_like(edge)

    @pl.when(dev < 255)
    def _():
        pltpu.make_async_copy(edge, edge, erecv).wait()

    own = samples[...]
    following = jnp.where(
        iota((LANE, LANE), 0) == LANE - 1, edge[0:1, :], pltpu.roll(own, LANE - 1, 0)
    )
    for q in range(8):
        if q == 0:
            window = own
        elif q < 7:
            window = pltpu.roll(own, LANE - 16 * q, 1)
        else:
            window = jnp.where(
                iota((LANE, LANE), 1) < 16, pltpu.roll(own, 16, 1), pltpu.roll(following, 16, 1)
            )
        win[pl.ds(q, LANE, stride=8), :] = window

    def forward_block(r, carry):
        here = aligned(r * LANE, LANE, LANE)
        stem_out = dot3(split(win[here, :]), (swh[...], swl[...]))
        scale = lax.rsqrt(jnp.mean(stem_out * stem_out, axis=1, keepdims=True) + EPSILON)
        norm = stem_out * scale
        proj = dot3(split(norm), (iwh[...], iwl[...]))
        stem[here, :] = stem_out
        normed[here, :] = norm
        qkv[here, :] = proj
        put_rows(1, r, proj[:, CH : 2 * CH] * proj[:, 2 * CH :])
        return carry

    lax.fori_loop(0, 8, forward_block, 0)
    scatter_in(1)

    def grad_block(r, carry):
        here = aligned(r * LANE, LANE, LANE)
        gated_grad = dot3(split(cot[here, :]), (owh[...], owl[...]), mm_nt)
        gg[here, :] = gated_grad
        put_rows(2, r, gated_grad * qkv[here, 0:CH])
        return carry

    lax.fori_loop(0, 8, grad_block, 0)
    scatter_in(2)

    def f1_block(b, carry):
        k1 = iota((16, FR), 0) + b * 16
        c, s = sincos(iota((16, FR), 1) * (2 * k1 + core), 2048)
        h, l = split(c)
        f1h[aligned(b * 16, 16, 16), :] = h
        f1l[aligned(b * 16, 16, 16), :] = l
        h, l = split(-s)
        f1h[aligned(512 + b * 16, 16, 16), :] = h
        f1l[aligned(512 + b * 16, 16, 16), :] = l
        return carry

    lax.fori_loop(0, 32, f1_block, 0)

    def tw_block(b, carry):
        here = aligned(b * 16, 16, 16)
        k1 = iota((16, LANE), 0) + b * 16
        c, s = sincos(iota((16, LANE), 1) * (2 * k1 + core), 2 * HALF)
        twc[here, :] = c
        tws[here, :] = -s
        return carry

    lax.fori_loop(0, ROWS // 16, tw_block, 0)

    cc, ss = sincos(iota((LANE, LANE), 0) * iota((LANE, LANE), 1), LANE)
    for (i, j), fwd, inv in (((0, 0), cc, cc), ((0, 1), -ss, ss), ((1, 0), ss, -ss), ((1, 1), cc, cc)):
        box = (slice(i * LANE, (i + 1) * LANE), slice(j * LANE, (j + 1) * LANE))
        w2h[box], w2l[box] = split(fwd)
        v2h[box], v2l[box] = split(inv)

    def g_block(b, carry):
        here = aligned(b * 16, 16, 16)
        n1 = iota((16, 512), 0) + b * 16
        c, s = sincos(n1 * (2 * iota((16, 512), 1) + core), 2048)
        gh[here, 0:512], gl[here, 0:512] = split(c)
        gh[here, 512:], gl[here, 512:] = split(-s)
        return carry

    lax.fori_loop(0, FR // 16, g_block, 0)

    odd = (1 - 2 * (iota((FR, LANE), 0) % 2)).astype(F32)

    def exchange(src, slot):
        pltpu.make_async_remote_copy(
            src, xbuf[slot], xsend.at[slot], xrecv.at[slot],
            device_id=partner, device_id_type=MESH,
        ).start()

    def exchanged(slot):
        pltpu.make_async_copy(xbuf[slot], xbuf[slot], xrecv.at[slot]).wait()

    def table_product(high, low, b):
        here = aligned(b * 512, 512, 512)
        both = mm(high[here, :], rhs2[...])
        return both[:, :LANE] + (both[:, LANE:] + mm(low[here, :], rhs2[:, :LANE]))

    def transform(unit):
        arrived(rbuf[unit], unit)
        exchange(rbuf[unit], unit)
        exchanged(unit)
        data = xbuf[unit][...] + sign * rbuf[unit][...]
        h, l = split(data)
        rhs2[:, :LANE] = h
        rhs2[:, LANE:] = l
        middle = jnp.sum(data * odd, axis=0, keepdims=True)
        yr[512:, :] = jnp.where(iota((16, LANE), 0) == 0, middle, 0.0)
        yi[512:, :] = jnp.zeros((16, LANE), F32)
        yr[0:512, :] = table_product(f1h, f1l, 0)
        yi[0:512, :] = table_product(f1h, f1l, 1)

        def second(b, carry):
            here = aligned(b * CUT, CUT, 16)
            a, bb, c, s = yr[here, :], yi[here, :], twc[here, :], tws[here, :]
            turned = jnp.concatenate([a * c - bb * s, a * s + bb * c], axis=1)
            spec[unit, here, :] = dot3(split(turned), (w2h[...], w2l[...]))
            return carry

        lax.fori_loop(0, ROWS // CUT, second, 0)

    def inverse(unit, product):
        def second(b, carry):
            here = aligned(b * CUT, CUT, 16)
            z = dot3(split(product(here)), (v2h[...], v2l[...]))
            zr, zi = z[:, :LANE], z[:, LANE:]
            c, s = twc[here, :], tws[here, :]
            k1 = iota((CUT, LANE), 0) + b * CUT
            single = (k1 == 0) | (k1 == 512)
            weight = jnp.where(core == 0, jnp.where(single, 1.0, 2.0), jnp.where(k1 < 512, 2.0, 0.0))
            weight = weight * (2.0 ** -27)
            yr[here, :] = (zr * c + zi * s) * weight
            yi[here, :] = (zi * c - zr * s) * weight
            return carry

        lax.fori_loop(0, ROWS // CUT, second, 0)
        for part, base in ((yr, 0), (yi, 512)):
            h, l = split(part[0:512, :])
            rhs2[base : base + 512, :LANE] = h
            rhs2[base : base + 512, LANE:] = l
        middle = yr[512:513, :]
        for b in range(2):
            here = slice(b * 512, (b + 1) * 512)
            cbuf[unit][here, :] = table_product(gh, gl, b) + odd[here, :] * middle
        exchange(cbuf[unit], 3 + unit)
        exchanged(3 + unit)
        hbuf[unit][...] = xbuf[3 + unit][...] + sign * cbuf[unit][...]
        scatter_out(unit)

    def times(a, b, here):
        x, y = spec[a, here, :], spec[b, here, :]
        ar, ai, br, bi = x[:, :LANE], x[:, LANE:], y[:, :LANE], y[:, LANE:]
        return ar, ai, br, bi

    def plain(a, b):
        def product(here):
            ar, ai, br, bi = times(a, b, here)
            return jnp.concatenate([ar * br - ai * bi, ar * bi + ai * br], axis=1)

        return product

    def conjugate(a, b):
        def product(here):
            ar, ai, br, bi = times(a, b, here)
            return jnp.concatenate([ar * br + ai * bi, ar * bi - ai * br], axis=1)

        return product

    transform(0)
    transform(1)
    inverse(0, plain(0, 1))
    transform(2)
    inverse(1, conjugate(0, 2))
    inverse(2, conjugate(1, 2))

    gsum[...] = jnp.zeros_like(gsum)

    def frames_of(unit, r):
        return obuf[unit][pl.ds(r, CH, stride=8), :].T

    arrived(obuf[0], 3)

    def conv_block(r, carry):
        here = aligned(r * LANE, LANE, LANE)
        conv = frames_of(0, r)
        gated = qkv[here, 0:CH] * conv
        layer_out[here, :] = dot3(split(gated), (owh[...], owl[...])) + stem[here, :]
        gsum[384:512, :] += dot3(split(gated.T), split(cot[here, :]))
        gg[here, :] = gg[here, :] * conv
        return carry

    lax.fori_loop(0, 8, conv_block, 0)

    arrived(obuf[1], 4)

    def back_block(r, carry):
        here = aligned(r * LANE, LANE, LANE)
        input_grad = frames_of(1, r)
        norm = normed[here, :]
        proj_grad = split(
            jnp.concatenate(
                [gg[here, :], input_grad * qkv[here, 2 * CH :], input_grad * qkv[here, CH : 2 * CH]],
                axis=1,
            )
        )
        grads = dot3(split(norm.T), proj_grad)
        for i in range(3):
            gsum[i * CH : (i + 1) * CH, :] += grads[:, i * CH : (i + 1) * CH]
        normed_grad = dot3(proj_grad, (iwh[...], iwl[...]), mm_nt)
        stem_out = stem[here, :]
        scale = lax.rsqrt(jnp.mean(stem_out * stem_out, axis=1, keepdims=True) + EPSILON)
        along = jnp.mean(norm * normed_grad, axis=1, keepdims=True)
        stem_out_grad = cot[here, :] + scale * (normed_grad - norm * along)
        gsum[512:544, :] += dot3(split(win[here, :].T), split(stem_out_grad))[0:32, :]
        return carry

    lax.fori_loop(0, 8, back_block, 0)

    z, x_lo = row // 4, (row // 2) % 2
    first, second_place = z * 2 + core, x_lo * 8 + col

    def share(step, src, dst, own_place, target):
        def one(i, carry):
            m = (own_place + 1 + i) % MEMBERS
            pltpu.make_async_remote_copy(
                src(m), dst.at[own_place], rsend.at[step], rrecv.at[step],
                device_id=target(m), device_id_type=MESH,
            ).start()
            return carry

        lax.fori_loop(0, MEMBERS - 1, one, 0)
        pltpu.make_async_copy(src(own_place), dst.at[own_place], rrecv.at[step]).start()
        pltpu.make_async_copy(dst, dst, rrecv.at[step]).wait()

    def in_first(m):
        return ((m // 2) * 4 + x_lo * 2 + m % 2, col)

    def in_second(m):
        return (z * 4 + (m // 8) * 2 + core, m % 8)

    share(0, lambda m: gsum.at[aligned(m * PIECE, PIECE)], rs_in, first, in_first)
    red[...] = jnp.sum(rs_in[...], axis=0)
    share(1, lambda m: red, ag_in, second_place, in_second)
    tot[...] = jnp.sum(ag_in[...], axis=0) * (2.0 ** -9)
    share(2, lambda m: tot, fin, first, in_first)

    def summed(start, size, out, columns):
        done = 0
        while done < size:
            piece, offset = divmod(start + done, PIECE)
            count = min(PIECE - offset, size - done)
            out[done : done + count, columns] = fin[piece, offset : offset + count, :]
            done += count

    for i in range(3):
        summed(i * CH, CH, in_grad, slice(i * CH, (i + 1) * CH))
    summed(384, CH, out_grad, slice(0, CH))
    summed(512, 32, stem_grad, slice(0, CH))

    arrived(obuf[2], 5)

    def filter_grad_block(r, carry):
        filter_grad[aligned(r * LANE, LANE, LANE), :] = frames_of(2, r)
        return carry

    lax.fori_loop(0, 8, filter_grad_block, 0)

    for unit in range(3):
        sent(sbuf[unit], unit)
        sent(hbuf[unit], 3 + unit)
        pltpu.make_async_copy(rbuf[unit], rbuf[unit], xsend.at[unit]).wait()
        pltpu.make_async_copy(cbuf[unit], cbuf[unit], xsend.at[3 + unit]).wait()
    for step in range(3):
        part = fin.at[pl.ds(0, MEMBERS - 1)]
        pltpu.make_async_copy(part, part, rsend.at[step]).wait()

    @pl.when(dev > 0)
    def _():
        pltpu.make_async_copy(edge, edge, esend).wait()


def body(samples, stem_weight, in_weight, filter_param, out_weight, cotangent):
    vmem = pl.BlockSpec(memory_space=pltpu.VMEM)
    stem_padded = jnp.pad(stem_weight, ((0, CH - stem_weight.shape[0]), (0, 0)))
    return pl.pallas_call(
        kernel,
        out_shape=(
            jax.ShapeDtypeStruct((FR, CH), F32),
            jax.ShapeDtypeStruct((FR, CH), F32),
            jax.ShapeDtypeStruct((32, CH), F32),
            jax.ShapeDtypeStruct((CH, 3 * CH), F32),
            jax.ShapeDtypeStruct((CH, CH), F32),
        ),
        in_specs=[vmem] * 6,
        out_specs=(vmem,) * 5,
        scratch_shapes=[
            *[pltpu.VMEM((FR, LANE), F32)] * 21,
            pltpu.VMEM((FR, FR), BF16), pltpu.VMEM((FR, FR), BF16),
            pltpu.VMEM((FR, FR), BF16), pltpu.VMEM((FR, FR), BF16),
            pltpu.VMEM((256, 256), BF16), pltpu.VMEM((256, 256), BF16),
            pltpu.VMEM((256, 256), BF16), pltpu.VMEM((256, 256), BF16),
            pltpu.VMEM((ROWS, LANE), F32), pltpu.VMEM((ROWS, LANE), F32),
            pltpu.VMEM((FR, 256), BF16),
            pltpu.VMEM((ROWS, LANE), F32), pltpu.VMEM((ROWS, LANE), F32),
            pltpu.VMEM((3, ROWS, 256), F32),
            pltpu.VMEM((8, LANE), F32),
            pltpu.VMEM((FR, LANE), F32), pltpu.VMEM((FR, LANE), F32), pltpu.VMEM((FR, LANE), F32),
            pltpu.VMEM((FR, 3 * CH), F32), pltpu.VMEM((FR, LANE), F32),
            pltpu.VMEM((CH, CH), BF16), pltpu.VMEM((CH, CH), BF16),
            pltpu.VMEM((CH, 3 * CH), BF16), pltpu.VMEM((CH, 3 * CH), BF16),
            pltpu.VMEM((CH, CH), BF16), pltpu.VMEM((CH, CH), BF16),
            pltpu.VMEM((MEMBERS * PIECE, LANE), F32), pltpu.VMEM((MEMBERS, PIECE, LANE), F32),
            pltpu.VMEM((PIECE, LANE), F32), pltpu.VMEM((MEMBERS, PIECE, LANE), F32),
            pltpu.VMEM((PIECE, LANE), F32), pltpu.VMEM((MEMBERS, PIECE, LANE), F32),
            pltpu.SemaphoreType.DMA((6,)), pltpu.SemaphoreType.DMA((6,)),
            pltpu.SemaphoreType.DMA((6,)), pltpu.SemaphoreType.DMA((6,)),
            pltpu.SemaphoreType.DMA, pltpu.SemaphoreType.DMA,
            pltpu.SemaphoreType.DMA((3,)), pltpu.SemaphoreType.DMA((3,)),
        ],
        compiler_params=pltpu.CompilerParams(has_side_effects=True, vmem_limit_bytes=60 * 2**20),
    )(samples.reshape(LANE, LANE), stem_padded, in_weight, filter_param, out_weight, cotangent)


def solution(mesh):
    in_specs = (P(("row", "col")), P(), P(), P(("row", "col"), None), P(), P(("row", "col"), None))
    out_specs = (P(("row", "col"), None), P(("row", "col"), None), P(), P(), P())
    return jax.shard_map(body, mesh=mesh, in_specs=in_specs, out_specs=out_specs, check_vma=False)
```

```python
import math

import jax
import jax.numpy as jnp
from jax import lax
from jax.experimental import pallas as pl
from jax.experimental.pallas import tpu as pltpu
from jax.sharding import PartitionSpec as P

MESH = pl.DeviceIdType.MESH
F32 = jnp.float32
BF16 = jnp.bfloat16
EPSILON = 1e-05

CH = 128
LANE = 128
FR = 1024
HALF = 131072
ROWS = 528
CUT = 176
PIECE = 40
MEMBERS = 16

COS_TERMS = [(-1.0) ** i / math.factorial(2 * i) for i in range(9)]
SIN_TERMS = [(-1.0) ** i / math.factorial(2 * i + 1) for i in range(9)]


def split(x):
    high = x.astype(BF16)
    return high, (x - high.astype(F32)).astype(BF16)


def mm(a, b):
    return jnp.dot(a, b, preferred_element_type=F32)


def mm_nt(a, b):
    return lax.dot_general(a, b, (((1,), (1,)), ((), ())), preferred_element_type=F32)


def dot3(a, b, form=mm):
    (ah, al), (bh, bl) = a, b
    return form(ah, bh) + (form(al, bh) + form(ah, bl))


def sincos(index, period):
    half = period // 2
    x = (((index + half) & (period - 1)) - half).astype(F32) * (2.0 * math.pi / period)
    x2 = x * x
    c = jnp.full_like(x, COS_TERMS[-1])
    s = jnp.full_like(x, SIN_TERMS[-1])
    for term in COS_TERMS[-2::-1]:
        c = c * x2 + term
    for term in SIN_TERMS[-2::-1]:
        s = s * x2 + term
    return c, s * x


def iota(shape, dim):
    return lax.broadcasted_iota(jnp.int32, shape, dim)


def aligned(start, size, unit=8):
    return pl.ds(pl.multiple_of(start, unit), size)


def kernel(
    samples, stem_w, in_w, filt, out_w, cot,
    rows_out, columns_out, sums,
    s0, s1, s2, r0, r1, r2, x0, x1, x2, x3, x4, x5, c0, c1, c2, h0, h1, h2, o0, o1, o2,
    f1h, f1l, gh, gl, w2h, w2l, v2h, v2l, twc, tws,
    rhs2, yr, yi, spec,
    edge, win, stem, normed, qkv, gg,
    swh, swl, iwh, iwl, owh, owl,
    gsum, rs_in, red, ag_in, tot, fin,
    send_sem, recv_sem, xsend, xrecv, esend, erecv, rsend, rrecv, known,
):
    sbuf, rbuf, xbuf = (s0, s1, s2), (r0, r1, r2), (x0, x1, x2, x3, x4, x5)
    cbuf, hbuf, obuf = (c0, c1, c2), (h0, h1, h2), (o0, o1, o2)
    row, col = lax.axis_index("row"), lax.axis_index("col")
    core = row % 2
    half = row // 16
    chip = (row // 2) * 8 + col
    place = (row % 16) * 8 + col
    dev = row * 8 + col
    partner = (row + 1 - 2 * core, col)
    sign = (1 - 2 * core).astype(F32)
    own_half = half == core

    def tile(k):
        return aligned(k * 8, 8)

    def scatter(src, dst, unit, slot, own, target):
        def one(i, carry):
            k = (own + 1 + i) % CH
            pltpu.make_async_remote_copy(
                src.at[tile(k)], dst.at[tile(slot)], send_sem.at[unit], recv_sem.at[unit],
                device_id=target(k), device_id_type=MESH,
            ).start()
            return carry

        lax.fori_loop(0, CH - 1, one, 0)

        @pl.when(own_half)
        def _():
            pltpu.make_async_copy(src.at[tile(own)], dst.at[tile(slot)], recv_sem.at[unit]).start()

        @pl.when(jnp.logical_not(own_half))
        def _():
            pltpu.make_async_remote_copy(
                src.at[tile(own)], dst.at[tile(slot)], send_sem.at[unit], recv_sem.at[unit],
                device_id=target(own), device_id_type=MESH,
            ).start()

    def arrived(dst, unit):
        pltpu.make_async_copy(dst, dst, recv_sem.at[unit]).wait()

    def sent(src, unit):
        @pl.when(own_half)
        def _():
            part = src.at[pl.ds(0, FR - 8)]
            pltpu.make_async_copy(part, part, send_sem.at[unit]).wait()

        @pl.when(jnp.logical_not(own_half))
        def _():
            pltpu.make_async_copy(src, src, send_sem.at[unit]).wait()

    def to_chip(k):
        return ((k // 8) * 2 + half, k % 8)

    def to_frames(k):
        return (k // 8 + 16 * core, k % 8)

    def scatter_in(unit):
        scatter(sbuf[unit], rbuf[unit], unit, place, chip, to_chip)

    def scatter_out(unit):
        scatter(hbuf[unit], obuf[unit], 3 + unit, chip, place, to_frames)

    z, x_lo = row // 4, (row // 2) % 2
    first, second_place = z * 2 + core, x_lo * 8 + col

    def in_first(m):
        return ((m // 2) * 4 + x_lo * 2 + m % 2, col)

    def in_second(m):
        return (z * 4 + (m // 8) * 2 + core, m % 8)

    def make_tables():
        def f1_block(b, carry):
            k1 = iota((16, FR), 0) + b * 16
            c, s = sincos(iota((16, FR), 1) * (2 * k1 + core), 2048)
            h, l = split(c)
            f1h[aligned(b * 16, 16, 16), :] = h
            f1l[aligned(b * 16, 16, 16), :] = l
            h, l = split(-s)
            f1h[aligned(512 + b * 16, 16, 16), :] = h
            f1l[aligned(512 + b * 16, 16, 16), :] = l
            return carry

        lax.fori_loop(0, 32, f1_block, 0)

        def tw_block(b, carry):
            here = aligned(b * 16, 16, 16)
            k1 = iota((16, LANE), 0) + b * 16
            c, s = sincos(iota((16, LANE), 1) * (2 * k1 + core), 2 * HALF)
            twc[here, :] = c
            tws[here, :] = -s
            return carry

        lax.fori_loop(0, ROWS // 16, tw_block, 0)

        cc, ss = sincos(iota((LANE, LANE), 0) * iota((LANE, LANE), 1), LANE)
        for (i, j), fwd, inv in (((0, 0), cc, cc), ((0, 1), -ss, ss), ((1, 0), ss, -ss), ((1, 1), cc, cc)):
            box = (slice(i * LANE, (i + 1) * LANE), slice(j * LANE, (j + 1) * LANE))
            w2h[box], w2l[box] = split(fwd)
            v2h[box], v2l[box] = split(inv)

        def g_block(b, carry):
            here = aligned(b * 16, 16, 16)
            n1 = iota((16, 512), 0) + b * 16
            c, s = sincos(n1 * (2 * iota((16, 512), 1) + core), 2048)
            gh[here, 0:512], gl[here, 0:512] = split(c)
            gh[here, 512:], gl[here, 512:] = split(-s)
            return carry

        lax.fori_loop(0, FR // 16, g_block, 0)

    barrier = pltpu.get_barrier_semaphore()

    def greet(i, carry):
        pl.semaphore_signal(
            barrier, 1, device_id=in_first((first + 1 + i) % MEMBERS), device_id_type=MESH
        )
        pl.semaphore_signal(
            barrier, 1, device_id=in_second((second_place + 1 + i) % MEMBERS), device_id_type=MESH
        )
        return carry

    lax.fori_loop(0, MEMBERS - 1, greet, 0)

    def put_rows(unit, r, block):
        sbuf[unit][pl.ds(r, CH, stride=8), :] = block.T

    def filter_block(r, carry):
        put_rows(0, r, filt[aligned(r * LANE, LANE, LANE), :])
        return carry

    lax.fori_loop(0, 8, filter_block, 0)

    for part in (swh, swl):
        part[...] = jnp.zeros_like(part)
    h, l = split(stem_w[...])
    swh[0:32, :] = h
    swl[0:32, :] = l
    for src, high, low in ((in_w, iwh, iwl), (out_w, owh, owl)):
        h, l = split(src[...])
        high[...] = h
        low[...] = l

    pl.semaphore_wait(barrier, 2 * (MEMBERS - 1))

    def confirm(i, carry):
        pl.semaphore_signal(
            known, 1, device_id=in_second((second_place + 1 + i) % MEMBERS), device_id_type=MESH
        )
        return carry

    lax.fori_loop(0, MEMBERS - 1, confirm, 0)
    make_tables()
    pl.semaphore_wait(known, MEMBERS - 1)

    @pl.when(dev > 0)
    def _():
        pltpu.make_async_remote_copy(
            samples.at[pl.ds(0, 8)], edge, esend, erecv,
            device_id=((dev - 1) // 8, (dev + 7) % 8), device_id_type=MESH,
        ).start()

    scatter_in(0)

    @pl.when(dev == 255)
    def _():
        edge[...] = jnp.zeros_like(edge)

    @pl.when(dev < 255)
    def _():
        pltpu.make_async_copy(edge, edge, erecv).wait()

    own = samples[...]
    following = jnp.where(
        iota((LANE, LANE), 0) == LANE - 1, edge[0:1, :], pltpu.roll(own, LANE - 1, 0)
    )
    for q in range(8):
        if q == 0:
            window = own
        elif q < 7:
            window = pltpu.roll(own, LANE - 16 * q, 1)
        else:
            window = jnp.where(
                iota((LANE, LANE), 1) < 16, pltpu.roll(own, 16, 1), pltpu.roll(following, 16, 1)
            )
        win[pl.ds(q, LANE, stride=8), :] = window

    def forward_block(r, carry):
        here = aligned(r * LANE, LANE, LANE)
        stem_out = dot3(split(win[here, :]), (swh[...], swl[...]))
        scale = lax.rsqrt(jnp.mean(stem_out * stem_out, axis=1, keepdims=True) + EPSILON)
        norm = stem_out * scale
        proj = dot3(split(norm), (iwh[...], iwl[...]))
        stem[here, :] = stem_out
        normed[here, :] = norm
        qkv[here, :] = proj
        put_rows(1, r, proj[:, CH : 2 * CH] * proj[:, 2 * CH :])
        return carry

    lax.fori_loop(0, 8, forward_block, 0)
    scatter_in(1)

    def grad_block(r, carry):
        here = aligned(r * LANE, LANE, LANE)
        gated_grad = dot3(split(cot[here, :]), (owh[...], owl[...]), mm_nt)
        gg[here, :] = gated_grad
        put_rows(2, r, gated_grad * qkv[here, 0:CH])
        return carry

    lax.fori_loop(0, 8, grad_block, 0)
    scatter_in(2)

    odd = (1 - 2 * (iota((FR, LANE), 0) % 2)).astype(F32)

    def exchange(src, slot):
        pltpu.make_async_remote_copy(
            src, xbuf[slot], xsend.at[slot], xrecv.at[slot],
            device_id=partner, device_id_type=MESH,
        ).start()

    def exchanged(slot):
        pltpu.make_async_copy(xbuf[slot], xbuf[slot], xrecv.at[slot]).wait()

    def table_product(high, low, b):
        here = aligned(b * 512, 512, 512)
        both = mm(high[here, :], rhs2[...])
        return both[:, :LANE] + (both[:, LANE:] + mm(low[here, :], rhs2[:, :LANE]))

    def transform(unit):
        arrived(rbuf[unit], unit)
        exchange(rbuf[unit], unit)
        exchanged(unit)
        data = xbuf[unit][...] + sign * rbuf[unit][...]
        h, l = split(data)
        rhs2[:, :LANE] = h
        rhs2[:, LANE:] = l
        middle = jnp.sum(data * odd, axis=0, keepdims=True)
        yr[512:, :] = jnp.where(iota((16, LANE), 0) == 0, middle, 0.0)
        yi[512:, :] = jnp.zeros((16, LANE), F32)
        yr[0:512, :] = table_product(f1h, f1l, 0)
        yi[0:512, :] = table_product(f1h, f1l, 1)

        def second(b, carry):
            here = aligned(b * CUT, CUT, 16)
            a, bb, c, s = yr[here, :], yi[here, :], twc[here, :], tws[here, :]
            turned = jnp.concatenate([a * c - bb * s, a * s + bb * c], axis=1)
            spec[unit, here, :] = dot3(split(turned), (w2h[...], w2l[...]))
            return carry

        lax.fori_loop(0, ROWS // CUT, second, 0)

    def inverse(unit, product):
        def second(b, carry):
            here = aligned(b * CUT, CUT, 16)
            z = dot3(split(product(here)), (v2h[...], v2l[...]))
            zr, zi = z[:, :LANE], z[:, LANE:]
            c, s = twc[here, :], tws[here, :]
            k1 = iota((CUT, LANE), 0) + b * CUT
            single = (k1 == 0) | (k1 == 512)
            weight = jnp.where(core == 0, jnp.where(single, 1.0, 2.0), jnp.where(k1 < 512, 2.0, 0.0))
            weight = weight * (2.0 ** -27)
            yr[here, :] = (zr * c + zi * s) * weight
            yi[here, :] = (zi * c - zr * s) * weight
            return carry

        lax.fori_loop(0, ROWS // CUT, second, 0)
        for part, base in ((yr, 0), (yi, 512)):
            h, l = split(part[0:512, :])
            rhs2[base : base + 512, :LANE] = h
            rhs2[base : base + 512, LANE:] = l
        middle = yr[512:513, :]
        for b in range(2):
            here = slice(b * 512, (b + 1) * 512)
            cbuf[unit][here, :] = table_product(gh, gl, b) + odd[here, :] * middle
        exchange(cbuf[unit], 3 + unit)
        exchanged(3 + unit)
        hbuf[unit][...] = xbuf[3 + unit][...] + sign * cbuf[unit][...]
        scatter_out(unit)

    def times(a, b, here):
        x, y = spec[a, here, :], spec[b, here, :]
        ar, ai, br, bi = x[:, :LANE], x[:, LANE:], y[:, :LANE], y[:, LANE:]
        return ar, ai, br, bi

    def plain(a, b):
        def product(here):
            ar, ai, br, bi = times(a, b, here)
            return jnp.concatenate([ar * br - ai * bi, ar * bi + ai * br], axis=1)

        return product

    def conjugate(a, b):
        def product(here):
            ar, ai, br, bi = times(a, b, here)
            return jnp.concatenate([ar * br + ai * bi, ar * bi - ai * br], axis=1)

        return product

    transform(0)
    transform(1)
    inverse(0, plain(0, 1))
    transform(2)
    inverse(1, conjugate(0, 2))
    inverse(2, conjugate(1, 2))

    gsum[...] = jnp.zeros_like(gsum)

    def frames_of(unit, r):
        return obuf[unit][pl.ds(r, CH, stride=8), :].T

    arrived(obuf[0], 3)

    def conv_block(r, carry):
        here = aligned(r * LANE, LANE, LANE)
        conv = frames_of(0, r)
        gated = qkv[here, 0:CH] * conv
        rows_out[here, :] = dot3(split(gated), (owh[...], owl[...])) + stem[here, :]
        gsum[384:512, :] += dot3(split(gated.T), split(cot[here, :]))
        gg[here, :] = gg[here, :] * conv
        return carry

    lax.fori_loop(0, 8, conv_block, 0)

    arrived(obuf[1], 4)

    def back_block(r, carry):
        here = aligned(r * LANE, LANE, LANE)
        input_grad = frames_of(1, r)
        norm = normed[here, :]
        proj_grad = split(
            jnp.concatenate(
                [gg[here, :], input_grad * qkv[here, 2 * CH :], input_grad * qkv[here, CH : 2 * CH]],
                axis=1,
            )
        )
        grads = dot3(split(norm.T), proj_grad)
        for i in range(3):
            gsum[i * CH : (i + 1) * CH, :] += grads[:, i * CH : (i + 1) * CH]
        normed_grad = dot3(proj_grad, (iwh[...], iwl[...]), mm_nt)
        stem_out = stem[here, :]
        scale = lax.rsqrt(jnp.mean(stem_out * stem_out, axis=1, keepdims=True) + EPSILON)
        along = jnp.mean(norm * normed_grad, axis=1, keepdims=True)
        stem_out_grad = cot[here, :] + scale * (normed_grad - norm * along)
        gsum[512:544, :] += dot3(split(win[here, :].T), split(stem_out_grad))[0:32, :]
        return carry

    lax.fori_loop(0, 8, back_block, 0)

    def share(step, src, dst, own_place, target):
        def one(i, carry):
            m = (own_place + 1 + i) % MEMBERS
            pltpu.make_async_remote_copy(
                src(m), dst.at[own_place], rsend.at[step], rrecv.at[step],
                device_id=target(m), device_id_type=MESH,
            ).start()
            return carry

        lax.fori_loop(0, MEMBERS - 1, one, 0)
        pltpu.make_async_copy(src(own_place), dst.at[own_place], rrecv.at[step]).start()
        pltpu.make_async_copy(dst, dst, rrecv.at[step]).wait()

    share(0, lambda m: gsum.at[aligned(m * PIECE, PIECE)], rs_in, first, in_first)
    red[...] = jnp.sum(rs_in[...], axis=0)
    share(1, lambda m: red, ag_in, second_place, in_second)
    tot[...] = jnp.sum(ag_in[...], axis=0) * (2.0 ** -9)
    share(2, lambda m: tot, fin, first, in_first)

    for m in range(MEMBERS):
        sums[m * PIECE : (m + 1) * PIECE, :] = fin[m]

    arrived(obuf[2], 5)

    columns_out[...] = obuf[2][...]

    for unit in range(3):
        sent(sbuf[unit], unit)
        sent(hbuf[unit], 3 + unit)
        pltpu.make_async_copy(rbuf[unit], rbuf[unit], xsend.at[unit]).wait()
        pltpu.make_async_copy(cbuf[unit], cbuf[unit], xsend.at[3 + unit]).wait()
    for step in range(3):
        part = fin.at[pl.ds(0, MEMBERS - 1)]
        pltpu.make_async_copy(part, part, rsend.at[step]).wait()

    @pl.when(dev > 0)
    def _():
        pltpu.make_async_copy(edge, edge, esend).wait()


def finish(rows_in, columns_in, sums, layer_out, filter_grad, stem_grad, in_grad, out_grad):
    layer_out[...] = rows_in[...]

    def block(r, carry):
        filter_grad[aligned(r * LANE, LANE, LANE), :] = columns_in[pl.ds(r, CH, stride=8), :].T
        return carry

    lax.fori_loop(0, 8, block, 0)
    for i in range(3):
        in_grad[:, i * CH : (i + 1) * CH] = sums[i * CH : (i + 1) * CH, :]
    out_grad[...] = sums[384:512, :]
    stem_grad[...] = sums[512:544, :]


def body(samples, stem_weight, in_weight, filter_param, out_weight, cotangent):
    vmem = pl.BlockSpec(memory_space=pltpu.VMEM)
    parts = pl.pallas_call(
        kernel,
        out_shape=(
            jax.ShapeDtypeStruct((FR, CH), F32),
            jax.ShapeDtypeStruct((FR, CH), F32),
            jax.ShapeDtypeStruct((MEMBERS * PIECE, CH), F32),
        ),
        in_specs=[vmem] * 6,
        out_specs=(vmem,) * 3,
        scratch_shapes=[
            *[pltpu.VMEM((FR, LANE), F32)] * 21,
            pltpu.VMEM((FR, FR), BF16), pltpu.VMEM((FR, FR), BF16),
            pltpu.VMEM((FR, FR), BF16), pltpu.VMEM((FR, FR), BF16),
            pltpu.VMEM((256, 256), BF16), pltpu.VMEM((256, 256), BF16),
            pltpu.VMEM((256, 256), BF16), pltpu.VMEM((256, 256), BF16),
            pltpu.VMEM((ROWS, LANE), F32), pltpu.VMEM((ROWS, LANE), F32),
            pltpu.VMEM((FR, 256), BF16),
            pltpu.VMEM((ROWS, LANE), F32), pltpu.VMEM((ROWS, LANE), F32),
            pltpu.VMEM((3, ROWS, 256), F32),
            pltpu.VMEM((8, LANE), F32),
            pltpu.VMEM((FR, LANE), F32), pltpu.VMEM((FR, LANE), F32), pltpu.VMEM((FR, LANE), F32),
            pltpu.VMEM((FR, 3 * CH), F32), pltpu.VMEM((FR, LANE), F32),
            pltpu.VMEM((CH, CH), BF16), pltpu.VMEM((CH, CH), BF16),
            pltpu.VMEM((CH, 3 * CH), BF16), pltpu.VMEM((CH, 3 * CH), BF16),
            pltpu.VMEM((CH, CH), BF16), pltpu.VMEM((CH, CH), BF16),
            pltpu.VMEM((MEMBERS * PIECE, LANE), F32), pltpu.VMEM((MEMBERS, PIECE, LANE), F32),
            pltpu.VMEM((PIECE, LANE), F32), pltpu.VMEM((MEMBERS, PIECE, LANE), F32),
            pltpu.VMEM((PIECE, LANE), F32), pltpu.VMEM((MEMBERS, PIECE, LANE), F32),
            pltpu.SemaphoreType.DMA((6,)), pltpu.SemaphoreType.DMA((6,)),
            pltpu.SemaphoreType.DMA((6,)), pltpu.SemaphoreType.DMA((6,)),
            pltpu.SemaphoreType.DMA, pltpu.SemaphoreType.DMA,
            pltpu.SemaphoreType.DMA((3,)), pltpu.SemaphoreType.DMA((3,)),
            pltpu.SemaphoreType.REGULAR,
        ],
        compiler_params=pltpu.CompilerParams(collective_id=0, has_side_effects=True, vmem_limit_bytes=60 * 2**20),
    )(samples.reshape(LANE, LANE), stem_weight, in_weight, filter_param, out_weight, cotangent)
    return pl.pallas_call(
        finish,
        out_shape=(
            jax.ShapeDtypeStruct((FR, CH), F32),
            jax.ShapeDtypeStruct((FR, CH), F32),
            jax.ShapeDtypeStruct((32, CH), F32),
            jax.ShapeDtypeStruct((CH, 3 * CH), F32),
            jax.ShapeDtypeStruct((CH, CH), F32),
        ),
        in_specs=[vmem] * 3,
        out_specs=(vmem,) * 5,
    )(*parts)


def solution(mesh):
    in_specs = (P(("row", "col")), P(), P(), P(("row", "col"), None), P(), P(("row", "col"), None))
    out_specs = (P(("row", "col"), None), P(("row", "col"), None), P(), P(), P())
    return jax.shard_map(body, mesh=mesh, in_specs=in_specs, out_specs=out_specs, check_vma=False)
```

```python
import math

import jax
import jax.numpy as jnp
from jax import lax
from jax.experimental import pallas as pl
from jax.experimental.pallas import tpu as pltpu
from jax.sharding import PartitionSpec as P

MESH = pl.DeviceIdType.MESH
F32 = jnp.float32
BF16 = jnp.bfloat16
EPSILON = 1e-05

CH = 128
LANE = 128
FR = 1024
HALF = 131072
ROWS = 528
CUT = 176
PIECE = 24
OWNERS = 23
PLANE = 32
SLABS = 8
CHUNKS = (64, 96, 127)
MEMBERS = 16

COS_TERMS = [(-1.0) ** i / math.factorial(2 * i) for i in range(9)]
SIN_TERMS = [(-1.0) ** i / math.factorial(2 * i + 1) for i in range(9)]


def split(x):
    high = x.astype(BF16)
    return high, (x - high.astype(F32)).astype(BF16)


def mm(a, b):
    return jnp.dot(a, b, preferred_element_type=F32)


def mm_nt(a, b):
    return lax.dot_general(a, b, (((1,), (1,)), ((), ())), preferred_element_type=F32)


def dot3(a, b, form=mm):
    (ah, al), (bh, bl) = a, b
    return form(ah, bh) + (form(al, bh) + form(ah, bl))


def sincos(index, period):
    half = period // 2
    x = (((index + half) & (period - 1)) - half).astype(F32) * (2.0 * math.pi / period)
    x2 = x * x
    c = jnp.full_like(x, COS_TERMS[-1])
    s = jnp.full_like(x, SIN_TERMS[-1])
    for term in COS_TERMS[-2::-1]:
        c = c * x2 + term
    for term in SIN_TERMS[-2::-1]:
        s = s * x2 + term
    return c, s * x


def iota(shape, dim):
    return lax.broadcasted_iota(jnp.int32, shape, dim)


def aligned(start, size, unit=8):
    return pl.ds(pl.multiple_of(start, unit), size)


def kernel(
    samples, stem_w, in_w, filt, out_w, cot,
    rows_out, columns_out, sums,
    s0, s1, s2, r0, r1, r2, x0, x1, x2, x3, x4, x5, c0, c1, c2, h0, h1, h2, o0, o1, o2,
    f1h, f1l, gh, gl, w2h, w2l, v2h, v2l, twc, tws,
    rhs2, yr, yi, spec,
    edge, win, stem, normed, qkv, gg,
    swh, swl, iwh, iwl, owh, owl,
    gsum, rs_in, red, ag_in, tot, fin,
    send_sem, recv_sem, xsend, xrecv, esend, erecv, rsend, rrecv, known,
):
    sbuf, rbuf, xbuf = (s0, s1, s2), (r0, r1, r2), (x0, x1, x2, x3, x4, x5)
    cbuf, hbuf, obuf = (c0, c1, c2), (h0, h1, h2), (o0, o1, o2)
    row, col = lax.axis_index("row"), lax.axis_index("col")
    core = row % 2
    half = row // 16
    chip = (row // 2) * 8 + col
    place = (row % 16) * 8 + col
    dev = row * 8 + col
    partner = (row + 1 - 2 * core, col)
    sign = (1 - 2 * core).astype(F32)
    own_half = half == core

    def tile(k):
        return aligned(k * 8, 8)

    def scatter_some(src, dst, unit, slot, own, target, begin, end):
        def one(i, carry):
            k = (own + 1 + i) % CH
            pltpu.make_async_remote_copy(
                src.at[tile(k)], dst.at[tile(slot)], send_sem.at[unit], recv_sem.at[unit],
                device_id=target(k), device_id_type=MESH,
            ).start()
            return carry

        lax.fori_loop(begin, end, one, 0)

    def scatter(src, dst, unit, slot, own, target, begin=0):
        scatter_some(src, dst, unit, slot, own, target, begin, CH - 1)

        @pl.when(own_half)
        def _():
            pltpu.make_async_copy(src.at[tile(own)], dst.at[tile(slot)], recv_sem.at[unit]).start()

        @pl.when(jnp.logical_not(own_half))
        def _():
            pltpu.make_async_remote_copy(
                src.at[tile(own)], dst.at[tile(slot)], send_sem.at[unit], recv_sem.at[unit],
                device_id=target(own), device_id_type=MESH,
            ).start()

    def arrived(dst, unit):
        pltpu.make_async_copy(dst, dst, recv_sem.at[unit]).wait()

    def sent(src, unit):
        @pl.when(own_half)
        def _():
            part = src.at[pl.ds(0, FR - 8)]
            pltpu.make_async_copy(part, part, send_sem.at[unit]).wait()

        @pl.when(jnp.logical_not(own_half))
        def _():
            pltpu.make_async_copy(src, src, send_sem.at[unit]).wait()

    def to_chip(k):
        return ((k // 8) * 2 + half, k % 8)

    def to_frames(k):
        return (k // 8 + 16 * core, k % 8)

    def scatter_in(unit):
        scatter(sbuf[unit], rbuf[unit], unit, place, chip, to_chip)

    def scatter_out(unit, begin=0):
        scatter(hbuf[unit], obuf[unit], 3 + unit, chip, place, to_frames, begin)

    def scatter_out_some(unit, begin, end):
        scatter_some(hbuf[unit], obuf[unit], 3 + unit, chip, place, to_frames, begin, end)

    z, x_lo = row // 4, (row // 2) % 2
    first, second_place = z * 2 + core, x_lo * 8 + col

    def in_first(m):
        return ((m // 2) * 4 + x_lo * 2 + m % 2, col)

    def in_second(m):
        return (z * 4 + (m // 8) * 2 + core, m % 8)

    def make_tables():
        def f1_block(b, carry):
            k1 = iota((16, FR), 0) + b * 16
            c, s = sincos(iota((16, FR), 1) * (2 * k1 + core), 2048)
            h, l = split(c)
            f1h[aligned(b * 16, 16, 16), :] = h
            f1l[aligned(b * 16, 16, 16), :] = l
            h, l = split(-s)
            f1h[aligned(512 + b * 16, 16, 16), :] = h
            f1l[aligned(512 + b * 16, 16, 16), :] = l
            return carry

        lax.fori_loop(0, 32, f1_block, 0)

        def tw_block(b, carry):
            here = aligned(b * 16, 16, 16)
            k1 = iota((16, LANE), 0) + b * 16
            c, s = sincos(iota((16, LANE), 1) * (2 * k1 + core), 2 * HALF)
            twc[here, :] = c
            tws[here, :] = -s
            return carry

        lax.fori_loop(0, ROWS // 16, tw_block, 0)

        cc, ss = sincos(iota((LANE, LANE), 0) * iota((LANE, LANE), 1), LANE)
        for (i, j), fwd, inv in (((0, 0), cc, cc), ((0, 1), -ss, ss), ((1, 0), ss, -ss), ((1, 1), cc, cc)):
            box = (slice(i * LANE, (i + 1) * LANE), slice(j * LANE, (j + 1) * LANE))
            w2h[box], w2l[box] = split(fwd)
            v2h[box], v2l[box] = split(inv)

        def g_block(b, carry):
            here = aligned(b * 16, 16, 16)
            n1 = iota((16, 512), 0) + b * 16
            c, s = sincos(n1 * (2 * iota((16, 512), 1) + core), 2048)
            gh[here, 0:512], gl[here, 0:512] = split(c)
            gh[here, 512:], gl[here, 512:] = split(-s)
            return carry

        lax.fori_loop(0, FR // 16, g_block, 0)

    barrier = pltpu.get_barrier_semaphore()

    def greet(i, carry):
        pl.semaphore_signal(
            barrier, 1, device_id=in_first((first + 1 + i) % MEMBERS), device_id_type=MESH
        )
        pl.semaphore_signal(
            barrier, 1, device_id=in_second((second_place + 1 + i) % MEMBERS), device_id_type=MESH
        )
        return carry

    lax.fori_loop(0, MEMBERS - 1, greet, 0)

    def put_rows(unit, r, block):
        sbuf[unit][pl.ds(r, CH, stride=8), :] = block.T

    def filter_block(r, carry):
        put_rows(0, r, filt[aligned(r * LANE, LANE, LANE), :])
        return carry

    lax.fori_loop(0, 8, filter_block, 0)

    for part in (swh, swl):
        part[...] = jnp.zeros_like(part)
    h, l = split(stem_w[...])
    swh[0:32, :] = h
    swl[0:32, :] = l
    for src, high, low in ((in_w, iwh, iwl), (out_w, owh, owl)):
        h, l = split(src[...])
        high[...] = h
        low[...] = l

    pl.semaphore_wait(barrier, 2 * (MEMBERS - 1))

    def confirm(i, carry):
        pl.semaphore_signal(
            known, 1, device_id=in_second((second_place + 1 + i) % MEMBERS), device_id_type=MESH
        )
        return carry

    lax.fori_loop(0, MEMBERS - 1, confirm, 0)
    pl.semaphore_wait(known, MEMBERS - 1)

    @pl.when(dev > 0)
    def _():
        pltpu.make_async_remote_copy(
            samples.at[pl.ds(0, 8)], edge, esend, erecv,
            device_id=((dev - 1) // 8, (dev + 7) % 8), device_id_type=MESH,
        ).start()

    scatter_in(0)

    @pl.when(dev == 255)
    def _():
        edge[...] = jnp.zeros_like(edge)

    @pl.when(dev < 255)
    def _():
        pltpu.make_async_copy(edge, edge, erecv).wait()

    own = samples[...]
    following = jnp.where(
        iota((LANE, LANE), 0) == LANE - 1, edge[0:1, :], pltpu.roll(own, LANE - 1, 0)
    )
    for q in range(8):
        if q == 0:
            window = own
        elif q < 7:
            window = pltpu.roll(own, LANE - 16 * q, 1)
        else:
            window = jnp.where(
                iota((LANE, LANE), 1) < 16, pltpu.roll(own, 16, 1), pltpu.roll(following, 16, 1)
            )
        win[pl.ds(q, LANE, stride=8), :] = window

    def forward_block(r, carry):
        here = aligned(r * LANE, LANE, LANE)
        stem_out = dot3(split(win[here, :]), (swh[...], swl[...]))
        scale = lax.rsqrt(jnp.mean(stem_out * stem_out, axis=1, keepdims=True) + EPSILON)
        norm = stem_out * scale
        proj = dot3(split(norm), (iwh[...], iwl[...]))
        stem[here, :] = stem_out
        normed[here, :] = norm
        qkv[here, :] = proj
        put_rows(1, r, proj[:, CH : 2 * CH] * proj[:, 2 * CH :])
        return carry

    lax.fori_loop(0, 8, forward_block, 0)
    scatter_in(1)

    def grad_block(r, carry):
        here = aligned(r * LANE, LANE, LANE)
        gated_grad = dot3(split(cot[here, :]), (owh[...], owl[...]), mm_nt)
        gg[here, :] = gated_grad
        put_rows(2, r, gated_grad * qkv[here, 0:CH])
        return carry

    lax.fori_loop(0, 8, grad_block, 0)
    scatter_in(2)
    make_tables()

    odd = (1 - 2 * (iota((FR, LANE), 0) % 2)).astype(F32)

    def exchange(src, slot):
        pltpu.make_async_remote_copy(
            src, xbuf[slot], xsend.at[slot], xrecv.at[slot],
            device_id=partner, device_id_type=MESH,
        ).start()

    def exchanged(slot):
        pltpu.make_async_copy(xbuf[slot], xbuf[slot], xrecv.at[slot]).wait()

    def table_product(high, low, b):
        here = aligned(b * 512, 512, 512)
        both = mm(high[here, :], rhs2[...])
        return both[:, :LANE] + (both[:, LANE:] + mm(low[here, :], rhs2[:, :LANE]))

    def transform(unit):
        arrived(rbuf[unit], unit)
        exchange(rbuf[unit], unit)
        exchanged(unit)
        data = xbuf[unit][...] + sign * rbuf[unit][...]
        h, l = split(data)
        rhs2[:, :LANE] = h
        rhs2[:, LANE:] = l
        middle = jnp.sum(data * odd, axis=0, keepdims=True)
        yr[512:, :] = jnp.where(iota((16, LANE), 0) == 0, middle, 0.0)
        yi[512:, :] = jnp.zeros((16, LANE), F32)
        yr[0:512, :] = table_product(f1h, f1l, 0)
        yi[0:512, :] = table_product(f1h, f1l, 1)

        def second(b, carry):
            here = aligned(b * CUT, CUT, 16)
            a, bb, c, s = yr[here, :], yi[here, :], twc[here, :], tws[here, :]
            turned = jnp.concatenate([a * c - bb * s, a * s + bb * c], axis=1)
            spec[unit, here, :] = dot3(split(turned), (w2h[...], w2l[...]))
            return carry

        lax.fori_loop(0, ROWS // CUT, second, 0)

    def inverse(unit, product):
        def second(b, carry):
            here = aligned(b * CUT, CUT, 16)
            z = dot3(split(product(here)), (v2h[...], v2l[...]))
            zr, zi = z[:, :LANE], z[:, LANE:]
            c, s = twc[here, :], tws[here, :]
            k1 = iota((CUT, LANE), 0) + b * CUT
            single = (k1 == 0) | (k1 == 512)
            weight = jnp.where(core == 0, jnp.where(single, 1.0, 2.0), jnp.where(k1 < 512, 2.0, 0.0))
            weight = weight * (2.0 ** -27)
            yr[here, :] = (zr * c + zi * s) * weight
            yi[here, :] = (zi * c - zr * s) * weight
            return carry

        lax.fori_loop(0, ROWS // CUT, second, 0)
        for part, base in ((yr, 0), (yi, 512)):
            h, l = split(part[0:512, :])
            rhs2[base : base + 512, :LANE] = h
            rhs2[base : base + 512, LANE:] = l
        middle = yr[512:513, :]
        for b in range(2):
            here = slice(b * 512, (b + 1) * 512)
            cbuf[unit][here, :] = table_product(gh, gl, b) + odd[here, :] * middle
        exchange(cbuf[unit], 3 + unit)
        exchanged(3 + unit)
        hbuf[unit][...] = xbuf[3 + unit][...] + sign * cbuf[unit][...]

    def times(a, b, here):
        x, y = spec[a, here, :], spec[b, here, :]
        ar, ai, br, bi = x[:, :LANE], x[:, LANE:], y[:, :LANE], y[:, LANE:]
        return ar, ai, br, bi

    def plain(a, b):
        def product(here):
            ar, ai, br, bi = times(a, b, here)
            return jnp.concatenate([ar * br - ai * bi, ar * bi + ai * br], axis=1)

        return product

    def conjugate(a, b):
        def product(here):
            ar, ai, br, bi = times(a, b, here)
            return jnp.concatenate([ar * br + ai * bi, ar * bi - ai * br], axis=1)

        return product

    transform(0)
    transform(1)
    inverse(0, plain(0, 1))
    scatter_out(0)
    transform(2)
    inverse(1, conjugate(0, 2))
    scatter_out(1)
    inverse(2, conjugate(1, 2))
    scatter_out_some(2, 0, CHUNKS[0])

    gsum[...] = jnp.zeros_like(gsum)

    def frames_of(unit, r):
        return obuf[unit][pl.ds(r, CH, stride=8), :].T

    arrived(obuf[0], 3)

    def conv_block(r, carry):
        here = aligned(r * LANE, LANE, LANE)
        conv = frames_of(0, r)
        gated = qkv[here, 0:CH] * conv
        rows_out[here, :] = dot3(split(gated), (owh[...], owl[...])) + stem[here, :]
        gsum[384:512, :] += dot3(split(gated.T), split(cot[here, :]))
        gg[here, :] = gg[here, :] * conv
        return carry

    lax.fori_loop(0, 8, conv_block, 0)

    arrived(obuf[1], 4)

    def back_block(r, carry):
        here = aligned(r * LANE, LANE, LANE)
        input_grad = frames_of(1, r)
        norm = normed[here, :]
        proj_grad = split(
            jnp.concatenate(
                [gg[here, :], input_grad * qkv[here, 2 * CH :], input_grad * qkv[here, CH : 2 * CH]],
                axis=1,
            )
        )
        grads = dot3(split(norm.T), proj_grad)
        for i in range(3):
            gsum[i * CH : (i + 1) * CH, :] += grads[:, i * CH : (i + 1) * CH]
        normed_grad = dot3(proj_grad, (iwh[...], iwl[...]), mm_nt)
        stem_out = stem[here, :]
        scale = lax.rsqrt(jnp.mean(stem_out * stem_out, axis=1, keepdims=True) + EPSILON)
        along = jnp.mean(norm * normed_grad, axis=1, keepdims=True)
        stem_out_grad = cot[here, :] + scale * (normed_grad - norm * along)
        gsum[512:544, :] += dot3(split(win[here, :].T), split(stem_out_grad))[0:32, :]
        return carry

    lax.fori_loop(0, 8, back_block, 0)

    in_plane = (x_lo * 8 + col) * 2 + core
    owner = in_plane < OWNERS

    def plane_device(m):
        return (z * 4 + (m // 16) * 2 + m % 2, (m // 2) % 8)

    def slab_device(m):
        return (m * 4 + row % 4, col)

    def give(step, src, dst, target):
        pltpu.make_async_remote_copy(
            src, dst, rsend.at[step], rrecv.at[step], device_id=target, device_id_type=MESH
        ).start()

    def keep(step, src, dst):
        pltpu.make_async_copy(src, dst, rrecv.at[step]).start()

    def came(step, dst):
        pltpu.make_async_copy(dst, dst, rrecv.at[step]).wait()

    def give_piece(i, carry):
        m = (in_plane + i) % OWNERS
        src = gsum.at[aligned(m * PIECE, PIECE)]

        @pl.when(m == in_plane)
        def _():
            keep(0, src, rs_in.at[in_plane])

        @pl.when(m != in_plane)
        def _():
            give(0, src, rs_in.at[in_plane], plane_device(m))

        return carry

    lax.fori_loop(0, OWNERS, give_piece, 0)
    scatter_out_some(2, CHUNKS[0], CHUNKS[1])

    @pl.when(owner)
    def _():
        came(0, rs_in)
        red[...] = jnp.sum(rs_in[...], axis=0)

        def give_slab(i, carry):
            give(1, red, ag_in.at[z], slab_device((z + 1 + i) % SLABS))
            return carry

        lax.fori_loop(0, SLABS - 1, give_slab, 0)
        keep(1, red, ag_in.at[z])

    scatter_out_some(2, CHUNKS[1], CHUNKS[2])

    @pl.when(owner)
    def _():
        came(1, ag_in)
        tot[...] = jnp.sum(ag_in[...], axis=0) * (2.0 ** -9)

        def give_total(i, carry):
            give(2, tot, fin.at[in_plane], plane_device((in_plane + 1 + i) % PLANE))
            return carry

        lax.fori_loop(0, PLANE - 1, give_total, 0)
        keep(2, tot, fin.at[in_plane])

    scatter_out(2, CHUNKS[2])
    came(2, fin)
    for m in range(OWNERS):
        sums[m * PIECE : (m + 1) * PIECE, :] = fin[m]

    arrived(obuf[2], 5)

    columns_out[...] = obuf[2][...]

    for unit in range(3):
        sent(sbuf[unit], unit)
        sent(hbuf[unit], 3 + unit)
        pltpu.make_async_copy(rbuf[unit], rbuf[unit], xsend.at[unit]).wait()
        pltpu.make_async_copy(cbuf[unit], cbuf[unit], xsend.at[3 + unit]).wait()
    def left(step, ref):
        pltpu.make_async_copy(ref, ref, rsend.at[step]).wait()

    @pl.when(owner)
    def _():
        left(0, rs_in.at[pl.ds(0, OWNERS - 1)])
        left(1, ag_in.at[pl.ds(0, SLABS - 1)])
        left(2, rs_in.at[pl.ds(0, PLANE - 1)])

    @pl.when(jnp.logical_not(owner))
    def _():
        left(0, rs_in.at[pl.ds(0, OWNERS)])

    @pl.when(dev > 0)
    def _():
        pltpu.make_async_copy(edge, edge, esend).wait()


def finish(rows_in, columns_in, sums, layer_out, filter_grad, stem_grad, in_grad, out_grad):
    layer_out[...] = rows_in[...]

    def block(r, carry):
        filter_grad[aligned(r * LANE, LANE, LANE), :] = columns_in[pl.ds(r, CH, stride=8), :].T
        return carry

    lax.fori_loop(0, 8, block, 0)
    for i in range(3):
        in_grad[:, i * CH : (i + 1) * CH] = sums[i * CH : (i + 1) * CH, :]
    out_grad[...] = sums[384:512, :]
    stem_grad[...] = sums[512:544, :]


def body(samples, stem_weight, in_weight, filter_param, out_weight, cotangent):
    vmem = pl.BlockSpec(memory_space=pltpu.VMEM)
    parts = pl.pallas_call(
        kernel,
        out_shape=(
            jax.ShapeDtypeStruct((FR, CH), F32),
            jax.ShapeDtypeStruct((FR, CH), F32),
            jax.ShapeDtypeStruct((OWNERS * PIECE, CH), F32),
        ),
        in_specs=[vmem] * 6,
        out_specs=(vmem,) * 3,
        scratch_shapes=[
            *[pltpu.VMEM((FR, LANE), F32)] * 21,
            pltpu.VMEM((FR, FR), BF16), pltpu.VMEM((FR, FR), BF16),
            pltpu.VMEM((FR, FR), BF16), pltpu.VMEM((FR, FR), BF16),
            pltpu.VMEM((256, 256), BF16), pltpu.VMEM((256, 256), BF16),
            pltpu.VMEM((256, 256), BF16), pltpu.VMEM((256, 256), BF16),
            pltpu.VMEM((ROWS, LANE), F32), pltpu.VMEM((ROWS, LANE), F32),
            pltpu.VMEM((FR, 256), BF16),
            pltpu.VMEM((ROWS, LANE), F32), pltpu.VMEM((ROWS, LANE), F32),
            pltpu.VMEM((3, ROWS, 256), F32),
            pltpu.VMEM((8, LANE), F32),
            pltpu.VMEM((FR, LANE), F32), pltpu.VMEM((FR, LANE), F32), pltpu.VMEM((FR, LANE), F32),
            pltpu.VMEM((FR, 3 * CH), F32), pltpu.VMEM((FR, LANE), F32),
            pltpu.VMEM((CH, CH), BF16), pltpu.VMEM((CH, CH), BF16),
            pltpu.VMEM((CH, 3 * CH), BF16), pltpu.VMEM((CH, 3 * CH), BF16),
            pltpu.VMEM((CH, CH), BF16), pltpu.VMEM((CH, CH), BF16),
            pltpu.VMEM((OWNERS * PIECE, LANE), F32), pltpu.VMEM((PLANE, PIECE, LANE), F32),
            pltpu.VMEM((PIECE, LANE), F32), pltpu.VMEM((SLABS, PIECE, LANE), F32),
            pltpu.VMEM((PIECE, LANE), F32), pltpu.VMEM((OWNERS, PIECE, LANE), F32),
            pltpu.SemaphoreType.DMA((6,)), pltpu.SemaphoreType.DMA((6,)),
            pltpu.SemaphoreType.DMA((6,)), pltpu.SemaphoreType.DMA((6,)),
            pltpu.SemaphoreType.DMA, pltpu.SemaphoreType.DMA,
            pltpu.SemaphoreType.DMA((3,)), pltpu.SemaphoreType.DMA((3,)),
            pltpu.SemaphoreType.REGULAR,
        ],
        compiler_params=pltpu.CompilerParams(collective_id=0, has_side_effects=True, vmem_limit_bytes=60 * 2**20),
    )(samples.reshape(LANE, LANE), stem_weight, in_weight, filter_param, out_weight, cotangent)
    return pl.pallas_call(
        finish,
        out_shape=(
            jax.ShapeDtypeStruct((FR, CH), F32),
            jax.ShapeDtypeStruct((FR, CH), F32),
            jax.ShapeDtypeStruct((32, CH), F32),
            jax.ShapeDtypeStruct((CH, 3 * CH), F32),
            jax.ShapeDtypeStruct((CH, CH), F32),
        ),
        in_specs=[vmem] * 3,
        out_specs=(vmem,) * 5,
    )(*parts)


def solution(mesh):
    in_specs = (P(("row", "col")), P(), P(), P(("row", "col"), None), P(), P(("row", "col"), None))
    out_specs = (P(("row", "col"), None), P(("row", "col"), None), P(), P(), P())
    return jax.shard_map(body, mesh=mesh, in_specs=in_specs, out_specs=out_specs, check_vma=False)
```
